32 devices in a mesh: layer: 8 (over z, x), land: 4 (over y, core).
Axes of the slice: x: 2, y: 2, z: 4, core: 2. Of those that a mesh axis runs over, the one named last changes fastest.
Arguments:
- gradients: bfloat16 [960, 65536], P(None, ('layer', 'land')), may hold values from -6 to 6
- queries: bfloat16 [32, 65536], P(None, ('layer', 'land')), may hold values from -6 to 6
- landmarks: bfloat16 [1024, 65536], P(None, ('layer', 'land')), may hold values from -0.0234375 to 0.0234375
- whitening: bfloat16 [1024, 1024], P(None, 'land'), may hold values from -2.5 to 2.5
Outputs:
- scores: float32 [32, 960], P('land', 'layer')
The draws below stay inside these ranges and needn't reach their ends.
All inputs are finite; a program needn't handle non-finite values.
Results may differ from the reference program's by a relative error of at most 0.023.
Values may be sent and summed in bfloat16 or wider, within the bound.
A program may use at most 128 MiB of HBM per device.

```python
import math
import jax
import jax.numpy as jnp

LANDMARKS = 1024
FEAT = 65536
ROWS = 960
NQ = 32


def draw_whitening(key, part):
    key_diag, key_off = jax.random.split(key)
    diagonal = jnp.exp(jax.random.uniform(key_diag, (LANDMARKS,), jnp.float32, math.log(0.5), math.log(2.0)))
    offdiag = jax.random.normal(key_off, (LANDMARKS, LANDMARKS), jnp.float32) * (0.6 / math.sqrt(LANDMARKS))
    identity = jnp.eye(LANDMARKS, dtype=jnp.float32)
    return (offdiag + identity * diagonal[None, :]).astype(jnp.bfloat16)


def block_levels(own_key, shape, pieces, low, top_value):
    factor_of = 1.0
    for axis_at, blocks in pieces:
        steps = jax.random.uniform(jax.random.fold_in(jax.random.fold_in(own_key, 6), axis_at), (blocks,), jnp.float32, low / len(pieces), top_value / len(pieces))
        factor_of = factor_of * jnp.repeat(jnp.exp(steps), shape[axis_at] // blocks).reshape((-1,) + (1,) * (len(shape) - 1 - axis_at))
    return factor_of


def noise(stream_key, dims, spread, limit, pieces=(), kind=jnp.bfloat16):
    drawn = spread * jax.random.normal(stream_key, dims, jnp.float32)
    if pieces:
        drawn = drawn * block_levels(stream_key, dims, pieces, -0.22, 0.18)
    return jnp.clip(drawn, -limit, limit).astype(kind)


def setup_inputs(seed: int = 0) -> dict:
    seeds = jax.random.split(jax.random.key(seed), 5)
    return {
        "gradients": noise(seeds[0], (ROWS, FEAT), 1.0, 6.0, ((1, 32),)),
        "queries": noise(seeds[1], (NQ, FEAT), 1.0, 6.0, ((1, 32),)),
        "landmarks": noise(seeds[2], (LANDMARKS, FEAT), FEAT ** -0.5, 0.0234375, ((1, 32),)),
        "whitening": draw_whitening(jax.random.fold_in(seeds[4], 71), 0),
    }


def reference(gradients, queries, landmarks, whitening):
    projected = jnp.dot(gradients, landmarks.T, preferred_element_type=jnp.float32).astype(jnp.bfloat16)
    query_proj = jnp.dot(queries, landmarks.T, preferred_element_type=jnp.float32).astype(jnp.bfloat16)
    whitened = jnp.dot(projected, whitening, preferred_element_type=jnp.float32).astype(jnp.bfloat16)
    query_white = jnp.dot(query_proj, whitening, preferred_element_type=jnp.float32).astype(jnp.bfloat16)
    scores = jnp.dot(query_white, whitened.T, preferred_element_type=jnp.float32)
    return scores * (LANDMARKS ** -0.5)
```

```python
import jax
import jax.numpy as jnp
from jax import lax
from jax.sharding import PartitionSpec as P

NN = (((1,), (0,)), ((), ()))
NT = (((1,), (1,)), ((), ()))


def dot(a, b, dims):
    return lax.dot_general(a, b, dims, preferred_element_type=jnp.float32)


def local(gradients, queries, landmarks, whitening):
    half = jnp.bfloat16
    factor = landmarks.shape[0] ** (-0.5)
    partial = dot(queries, landmarks, NT).astype(half)
    query_proj = lax.psum(partial, ("layer", "land"))
    query_white = dot(query_proj, whitening, NN).astype(half)
    back = lax.psum(dot(query_white, whitening, NT).astype(half), "land")
    spread = dot(back, landmarks, NN).astype(half)
    scores = dot(spread, gradients, NT) * factor
    share = lax.psum_scatter(
        scores.astype(half), "layer", scatter_dimension=1, tiled=True
    )
    return lax.psum_scatter(share, "land", scatter_dimension=0, tiled=True).astype(
        jnp.float32
    )


def solution(mesh):
    return jax.shard_map(
        local,
        mesh=mesh,
        in_specs=(
            P(None, ("layer", "land")),
            P(None, ("layer", "land")),
            P(None, ("layer", "land")),
            P(None, "land"),
        ),
        out_specs=P("land", "layer"),
        check_vma=False,
    )
```

```python
import functools
import jax
import jax.numpy as jnp
from jax import lax
from jax.experimental import pallas as pl
from jax.experimental.pallas import tpu as pltpu
from jax.sharding import PartitionSpec as P

NN = (((1,), (0,)), ((), ()))
NT = (((1,), (1,)), ((), ()))
HALF = jnp.bfloat16
FULL = jnp.float32


def dot(a, b, dims):
    return lax.dot_general(a, b, dims, preferred_element_type=FULL)


def kernel(
    n_layer, n_land, factor,
    g_hbm, q_hbm, l_hbm, w_hbm, out_ref,
    g_buf, q_buf, l_buf, w_buf, load_sem,
    qs, qr, hs, hr, us, ur, bs, br, ss, sr, fs, fr,
    layer_send, layer_recv, land_send, land_recv,
):
    layer = lax.axis_index("layer")
    land = lax.axis_index("land")
    n_blocks = l_buf.shape[0]

    loads = [pltpu.make_async_copy(q_hbm, q_buf, load_sem.at[0])]
    for b in range(n_blocks):
        loads.append(pltpu.make_async_copy(l_hbm.at[b], l_buf.at[b], load_sem.at[1 + b]))
    loads.append(pltpu.make_async_copy(w_hbm, w_buf, load_sem.at[1 + n_blocks]))
    loads.append(pltpu.make_async_copy(g_hbm, g_buf, load_sem.at[2 + n_blocks]))
    for load in loads:
        load.start()

    def layer_peer(k):
        return lax.rem(layer + k, n_layer)

    def land_peer(k):
        return lax.rem(land + k, n_land)

    barrier = pltpu.get_barrier_semaphore()
    for k in range(1, n_layer):
        pl.semaphore_signal(barrier, inc=1, device_id=(layer_peer(k), land),
                            device_id_type=pl.DeviceIdType.MESH)
    for k in range(1, n_land):
        pl.semaphore_signal(barrier, inc=1, device_id=(layer, land_peer(k)),
                            device_id_type=pl.DeviceIdType.MESH)

    def over_layer(phase, source, target):
        copies = []
        for k in range(1, n_layer):
            peer = layer_peer(k)
            copy = pltpu.make_async_remote_copy(
                src_ref=source(peer), dst_ref=target(k),
                send_sem=layer_send.at[phase, k - 1],
                recv_sem=layer_recv.at[phase, k - 1],
                device_id=(peer, land), device_id_type=pl.DeviceIdType.MESH)
            copy.start()
            copies.append(copy)
        return copies

    def over_land(phase, source, target):
        copies = []
        for k in range(1, n_land):
            peer = land_peer(k)
            copy = pltpu.make_async_remote_copy(
                src_ref=source(peer), dst_ref=target(k),
                send_sem=land_send.at[phase, k - 1],
                recv_sem=land_recv.at[phase, k - 1],
                device_id=(layer, peer), device_id_type=pl.DeviceIdType.MESH)
            copy.start()
            copies.append(copy)
        return copies

    sent = []

    loads[0].wait()
    rows = qs.shape[1]
    width = l_buf.shape[1]
    for b in range(n_blocks):
        loads[1 + b].wait()
        part = dot(q_buf[...], l_buf[b], NT)
        for i in range(n_layer):
            qs[i, :, b * width:(b + 1) * width] = part[i * rows:(i + 1) * rows].astype(HALF)

    pl.semaphore_wait(barrier, n_layer + n_land - 2)

    copies = over_layer(0, lambda p: qs.at[p], lambda k: qr.at[k - 1])
    total = qs[layer].astype(FULL)
    for k, copy in enumerate(copies):
        copy.wait_recv()
        total += qr[k].astype(FULL)
    sent += copies

    hs[...] = total
    copies = over_land(0, lambda p: hs, lambda k: hr.at[k - 1])
    for k, copy in enumerate(copies):
        copy.wait_recv()
        total += hr[k]
    sent += copies

    loads[1 + n_blocks].wait()
    white = dot(total.astype(HALF), w_buf[...], NN).astype(HALF)
    back = dot(white, w_buf[...], NT)
    us[...] = back
    copies = over_land(1, lambda p: us, lambda k: ur.at[k - 1])
    for k, copy in enumerate(copies):
        copy.wait_recv()
        back += ur[k]
    sent += copies

    bs[...] = back.astype(HALF)
    copies = over_layer(1, lambda p: bs, lambda k: br.at[layer])
    br[layer] = bs[...]
    loads[2 + n_blocks].wait()
    for copy in copies:
        copy.wait_recv()
    sent += copies

    folded = jnp.concatenate([br[i].astype(FULL) for i in range(n_layer)], axis=0).astype(HALF)
    spread = jnp.zeros((folded.shape[0], l_buf.shape[2]), FULL)
    for b in range(n_blocks):
        spread += dot(folded[:, b * width:(b + 1) * width], l_buf[b], NN)
    spread = spread.astype(HALF)

    for i in range(n_layer):
        ss[i] = (dot(spread, g_buf[i], NT) * factor).astype(HALF)
    copies = over_layer(2, lambda p: ss.at[p], lambda k: sr.at[k - 1])
    score = ss[layer].astype(FULL)
    for k, copy in enumerate(copies):
        copy.wait_recv()
        score += sr[k].astype(FULL)
    sent += copies

    share = fs.shape[1]
    for j in range(n_land):
        fs[j] = score[j * share:(j + 1) * share]
    copies = over_land(2, lambda p: fs.at[p], lambda k: fr.at[k - 1])
    result = fs[land]
    for k, copy in enumerate(copies):
        copy.wait_recv()
        result += fr[k]
    sent += copies
    out_ref[...] = result

    for copy in sent:
        copy.wait_send()


def fused(gradients, queries, landmarks, whitening):
    n_layer = lax.axis_size("layer")
    n_land = lax.axis_size("land")
    n_rows, width = gradients.shape
    n_query = queries.shape[0]
    n_mark = landmarks.shape[0]
    n_blocks = 4
    each, rows, share = n_rows // n_layer, n_query // n_layer, n_query // n_land
    any_space = pl.BlockSpec(memory_space=pl.ANY)
    return pl.pallas_call(
        functools.partial(kernel, n_layer, n_land, n_mark ** (-0.5)),
        out_shape=jax.ShapeDtypeStruct((share, each), FULL),
        in_specs=[any_space] * 4,
        out_specs=pl.BlockSpec(memory_space=pltpu.VMEM),
        scratch_shapes=[
            pltpu.VMEM((n_layer, each, width), HALF),
            pltpu.VMEM((n_query, width), HALF),
            pltpu.VMEM((n_blocks, n_mark // n_blocks, width), HALF),
            pltpu.VMEM(whitening.shape, HALF),
            pltpu.SemaphoreType.DMA((n_blocks + 3,)),
            pltpu.VMEM((n_layer, rows, n_mark), HALF),
            pltpu.VMEM((n_layer - 1, rows, n_mark), HALF),
            pltpu.VMEM((rows, n_mark), FULL),
            pltpu.VMEM((n_land - 1, rows, n_mark), FULL),
            pltpu.VMEM((rows, n_mark), FULL),
            pltpu.VMEM((n_land - 1, rows, n_mark), FULL),
            pltpu.VMEM((rows, n_mark), HALF),
            pltpu.VMEM((n_layer, rows, n_mark), HALF),
            pltpu.VMEM((n_layer, n_query, each), HALF),
            pltpu.VMEM((n_layer - 1, n_query, each), HALF),
            pltpu.VMEM((n_land, share, each), FULL),
            pltpu.VMEM((n_land - 1, share, each), FULL),
            pltpu.SemaphoreType.DMA((3, n_layer - 1)),
            pltpu.SemaphoreType.DMA((3, n_layer - 1)),
            pltpu.SemaphoreType.DMA((3, n_land - 1)),
            pltpu.SemaphoreType.DMA((3, n_land - 1)),
        ],
        compiler_params=pltpu.CompilerParams(
            collective_id=0, has_side_effects=True, vmem_limit_bytes=48 << 20
        ),
    )(
        gradients.reshape(n_layer, each, width),
        queries,
        landmarks.reshape(n_blocks, n_mark // n_blocks, width),
        whitening,
    )


def staged(gradients, queries, landmarks, whitening):
    factor = landmarks.shape[0] ** (-0.5)
    partial = dot(queries, landmarks, NT).astype(HALF)
    query_proj = lax.psum(partial, ("layer", "land"))
    query_white = dot(query_proj, whitening, NN).astype(HALF)
    back = lax.psum(dot(query_white, whitening, NT).astype(HALF), "land")
    spread = dot(back, landmarks, NN).astype(HALF)
    scores = dot(spread, gradients, NT) * factor
    share = lax.psum_scatter(
        scores.astype(HALF), "layer", scatter_dimension=1, tiled=True
    )
    return lax.psum_scatter(share, "land", scatter_dimension=0, tiled=True).astype(FULL)


def local(gradients, queries, landmarks, whitening):
    held = 2 * (gradients.size + queries.size + landmarks.size + whitening.size)
    few = lax.axis_size("layer") * lax.axis_size("land") <= 64
    if few and held <= (24 << 20) and gradients.shape[1] % 128 == 0:
        return fused(gradients, queries, landmarks, whitening)
    return staged(gradients, queries, landmarks, whitening)


def solution(mesh):
    return jax.shard_map(
        local,
        mesh=mesh,
        in_specs=(
            P(None, ("layer", "land")),
            P(None, ("layer", "land")),
            P(None, ("layer", "land")),
            P(None, "land"),
        ),
        out_specs=P("land", "layer"),
        check_vma=False,
    )
```

```python
import functools
import jax
import jax.numpy as jnp
from jax import lax
from jax.experimental import pallas as pl
from jax.experimental.pallas import tpu as pltpu
from jax.sharding import PartitionSpec as P

NN = (((1,), (0,)), ((), ()))
NT = (((1,), (1,)), ((), ()))
HALF = jnp.bfloat16
FULL = jnp.float32


def dot(a, b, dims):
    return lax.dot_general(a, b, dims, preferred_element_type=FULL)


def kernel(
    n_layer, n_land, factor,
    g_hbm, q_hbm, l_hbm, w_hbm, out_ref,
    g_buf, p_buf, q_buf, l_buf, w_buf, load_sem,
    qs, qr, hs, hr, us, ur, bs, br, ss, sr, fs, fr,
    layer_send, layer_recv, land_send, land_recv,
):
    layer = lax.axis_index("layer")
    land = lax.axis_index("land")
    n_blocks = l_buf.shape[0]

    loads = [pltpu.make_async_copy(q_hbm, q_buf, load_sem.at[0])]
    for b in range(n_blocks):
        loads.append(pltpu.make_async_copy(l_hbm.at[b], l_buf.at[b], load_sem.at[1 + b]))
    loads.append(pltpu.make_async_copy(w_hbm, w_buf, load_sem.at[1 + n_blocks]))
    loads.append(pltpu.make_async_copy(g_hbm, g_buf, load_sem.at[2 + n_blocks]))
    for load in loads:
        load.start()

    def layer_peer(k):
        return lax.rem(layer + k, n_layer)

    def land_peer(k):
        return lax.rem(land + k, n_land)

    barrier = pltpu.get_barrier_semaphore()
    for k in range(1, n_layer):
        pl.semaphore_signal(barrier, inc=1, device_id=(layer_peer(k), land),
                            device_id_type=pl.DeviceIdType.MESH)
    for k in range(1, n_land):
        pl.semaphore_signal(barrier, inc=1, device_id=(layer, land_peer(k)),
                            device_id_type=pl.DeviceIdType.MESH)

    def over_layer(phase, source, target):
        copies = []
        for k in range(1, n_layer):
            peer = layer_peer(k)
            copy = pltpu.make_async_remote_copy(
                src_ref=source(peer), dst_ref=target(k),
                send_sem=layer_send.at[phase, k - 1],
                recv_sem=layer_recv.at[phase, k - 1],
                device_id=(peer, land), device_id_type=pl.DeviceIdType.MESH)
            copy.start()
            copies.append(copy)
        return copies

    def over_land(phase, source, target):
        copies = []
        for k in range(1, n_land):
            peer = land_peer(k)
            copy = pltpu.make_async_remote_copy(
                src_ref=source(peer), dst_ref=target(k),
                send_sem=land_send.at[phase, k - 1],
                recv_sem=land_recv.at[phase, k - 1],
                device_id=(layer, peer), device_id_type=pl.DeviceIdType.MESH)
            copy.start()
            copies.append(copy)
        return copies

    sent = []
    each = p_buf.shape[1]

    def project(b):
        part = dot(g_buf[...], l_buf[b], NT)
        for i in range(n_layer):
            p_buf[i, :, b * width:(b + 1) * width] = part[i * each:(i + 1) * each].astype(HALF)

    loads[0].wait()
    rows = qs.shape[1]
    width = l_buf.shape[1]
    for b in range(n_blocks):
        loads[1 + b].wait()
        part = dot(q_buf[...], l_buf[b], NT)
        for i in range(n_layer):
            qs[i, :, b * width:(b + 1) * width] = part[i * rows:(i + 1) * rows].astype(HALF)

    pl.semaphore_wait(barrier, n_layer + n_land - 2)

    copies = over_layer(0, lambda p: qs.at[p], lambda k: qr.at[k - 1])
    loads[2 + n_blocks].wait()
    project(0)
    total = qs[layer].astype(FULL)
    for k, copy in enumerate(copies):
        copy.wait_recv()
        total += qr[k].astype(FULL)
    sent += copies

    hs[...] = total
    copies = over_land(0, lambda p: hs, lambda k: hr.at[k - 1])
    project(1)
    for k, copy in enumerate(copies):
        copy.wait_recv()
        total += hr[k]
    sent += copies

    loads[1 + n_blocks].wait()
    white = dot(total.astype(HALF), w_buf[...], NN).astype(HALF)
    back = dot(white, w_buf[...], NT)
    us[...] = back
    copies = over_land(1, lambda p: us, lambda k: ur.at[k - 1])
    project(2)
    for k, copy in enumerate(copies):
        copy.wait_recv()
        back += ur[k]
    sent += copies

    bs[...] = back.astype(HALF)
    copies = over_layer(1, lambda p: bs, lambda k: br.at[layer])
    br[layer] = bs[...]
    project(3)
    for copy in copies:
        copy.wait_recv()
    sent += copies

    folded = jnp.concatenate([br[i].astype(FULL) for i in range(n_layer)], axis=0).astype(HALF)
    for i in range(n_layer):
        ss[i] = (dot(folded, p_buf[i], NT) * factor).astype(HALF)
    copies = over_layer(2, lambda p: ss.at[p], lambda k: sr.at[k - 1])
    score = ss[layer].astype(FULL)
    for k, copy in enumerate(copies):
        copy.wait_recv()
        score += sr[k].astype(FULL)
    sent += copies

    share = fs.shape[1]
    for j in range(n_land):
        fs[j] = score[j * share:(j + 1) * share]
    copies = over_land(2, lambda p: fs.at[p], lambda k: fr.at[k - 1])
    result = fs[land]
    for k, copy in enumerate(copies):
        copy.wait_recv()
        result += fr[k]
    sent += copies
    out_ref[...] = result

    for copy in sent:
        copy.wait_send()


def fused(gradients, queries, landmarks, whitening):
    n_layer = lax.axis_size("layer")
    n_land = lax.axis_size("land")
    n_rows, width = gradients.shape
    n_query = queries.shape[0]
    n_mark = landmarks.shape[0]
    n_blocks = 4
    each, rows, share = n_rows // n_layer, n_query // n_layer, n_query // n_land
    any_space = pl.BlockSpec(memory_space=pltpu.HBM)
    return pl.pallas_call(
        functools.partial(kernel, n_layer, n_land, n_mark ** (-0.5)),
        out_shape=jax.ShapeDtypeStruct((share, each), FULL),
        in_specs=[any_space] * 4,
        out_specs=pl.BlockSpec(memory_space=pltpu.VMEM),
        scratch_shapes=[
            pltpu.VMEM((n_rows, width), HALF),
            pltpu.VMEM((n_layer, each, n_mark), HALF),
            pltpu.VMEM((n_query, width), HALF),
            pltpu.VMEM((n_blocks, n_mark // n_blocks, width), HALF),
            pltpu.VMEM(whitening.shape, HALF),
            pltpu.SemaphoreType.DMA((n_blocks + 3,)),
            pltpu.VMEM((n_layer, rows, n_mark), HALF),
            pltpu.VMEM((n_layer - 1, rows, n_mark), HALF),
            pltpu.VMEM((rows, n_mark), FULL),
            pltpu.VMEM((n_land - 1, rows, n_mark), FULL),
            pltpu.VMEM((rows, n_mark), FULL),
            pltpu.VMEM((n_land - 1, rows, n_mark), FULL),
            pltpu.VMEM((rows, n_mark), HALF),
            pltpu.VMEM((n_layer, rows, n_mark), HALF),
            pltpu.VMEM((n_layer, n_query, each), HALF),
            pltpu.VMEM((n_layer - 1, n_query, each), HALF),
            pltpu.VMEM((n_land, share, each), FULL),
            pltpu.VMEM((n_land - 1, share, each), FULL),
            pltpu.SemaphoreType.DMA((3, n_layer - 1)),
            pltpu.SemaphoreType.DMA((3, n_layer - 1)),
            pltpu.SemaphoreType.DMA((3, n_land - 1)),
            pltpu.SemaphoreType.DMA((3, n_land - 1)),
        ],
        compiler_params=pltpu.CompilerParams(
            collective_id=0, has_side_effects=True, vmem_limit_bytes=63 << 20
        ),
    )(
        gradients,
        queries,
        landmarks.reshape(n_blocks, n_mark // n_blocks, width),
        whitening,
    )


def staged(gradients, queries, landmarks, whitening):
    factor = landmarks.shape[0] ** (-0.5)
    partial = dot(queries, landmarks, NT).astype(HALF)
    query_proj = lax.psum(partial, ("layer", "land"))
    query_white = dot(query_proj, whitening, NN).astype(HALF)
    back = lax.psum(dot(query_white, whitening, NT).astype(HALF), "land")
    spread = dot(back, landmarks, NN).astype(HALF)
    scores = dot(spread, gradients, NT) * factor
    share = lax.psum_scatter(
        scores.astype(HALF), "layer", scatter_dimension=1, tiled=True
    )
    return lax.psum_scatter(share, "land", scatter_dimension=0, tiled=True).astype(FULL)


def local(gradients, queries, landmarks, whitening):
    held = 2 * (gradients.size + queries.size + landmarks.size + whitening.size)
    few = lax.axis_size("layer") * lax.axis_size("land") <= 64
    if few and held <= (24 << 20) and gradients.shape[1] % 128 == 0:
        return fused(gradients, queries, landmarks, whitening)
    return staged(gradients, queries, landmarks, whitening)


def solution(mesh):
    return jax.shard_map(
        local,
        mesh=mesh,
        in_specs=(
            P(None, ("layer", "land")),
            P(None, ("layer", "land")),
            P(None, ("layer", "land")),
            P(None, "land"),
        ),
        out_specs=P("land", "layer"),
        check_vma=False,
    )
```

```python
import functools
import jax
import jax.numpy as jnp
from jax import lax
from jax.experimental import pallas as pl
from jax.experimental.pallas import tpu as pltpu
from jax.sharding import PartitionSpec as P

NN = (((1,), (0,)), ((), ()))
NT = (((1,), (1,)), ((), ()))
HALF = jnp.bfloat16
FULL = jnp.float32


def dot(a, b, dims):
    return lax.dot_general(a, b, dims, preferred_element_type=FULL)


def kernel(
    n_layer, n_land, factor,
    g_hbm, q_hbm, l_hbm, w_hbm, out_ref,
    g_buf, p_buf, q_buf, l_buf, w_buf, load_sem,
    qs, qr, hs, hr, us, ur, bs, br, ss, sr,
    layer_send, layer_recv, land_send, land_recv, score_send, score_recv,
):
    layer = lax.axis_index("layer")
    land = lax.axis_index("land")
    n_blocks = l_buf.shape[0]

    loads = [pltpu.make_async_copy(q_hbm, q_buf, load_sem.at[0])]
    for b in range(n_blocks):
        loads.append(pltpu.make_async_copy(l_hbm.at[b], l_buf.at[b], load_sem.at[1 + b]))
    loads.append(pltpu.make_async_copy(w_hbm, w_buf, load_sem.at[1 + n_blocks]))
    loads.append(pltpu.make_async_copy(g_hbm, g_buf, load_sem.at[2 + n_blocks]))
    for load in loads:
        load.start()

    def layer_peer(k):
        return lax.rem(layer + k, n_layer)

    def land_peer(k):
        return lax.rem(land + k, n_land)

    barrier = pltpu.get_barrier_semaphore()
    for k in range(1, n_layer):
        pl.semaphore_signal(barrier, inc=1, device_id=(layer_peer(k), land),
                            device_id_type=pl.DeviceIdType.MESH)
    for k in range(1, n_land):
        pl.semaphore_signal(barrier, inc=1, device_id=(layer, land_peer(k)),
                            device_id_type=pl.DeviceIdType.MESH)

    def over_layer(phase, source, target):
        copies = []
        for k in range(1, n_layer):
            peer = layer_peer(k)
            copy = pltpu.make_async_remote_copy(
                src_ref=source(peer), dst_ref=target(k),
                send_sem=layer_send.at[phase, k - 1],
                recv_sem=layer_recv.at[phase, k - 1],
                device_id=(peer, land), device_id_type=pl.DeviceIdType.MESH)
            copy.start()
            copies.append(copy)
        return copies

    def over_land(phase, source, target):
        copies = []
        for k in range(1, n_land):
            peer = land_peer(k)
            copy = pltpu.make_async_remote_copy(
                src_ref=source(peer), dst_ref=target(k),
                send_sem=land_send.at[phase, k - 1],
                recv_sem=land_recv.at[phase, k - 1],
                device_id=(layer, peer), device_id_type=pl.DeviceIdType.MESH)
            copy.start()
            copies.append(copy)
        return copies

    sent = []
    each = p_buf.shape[1]

    def project(b):
        part = dot(g_buf[...], l_buf[b], NT)
        for i in range(n_layer):
            p_buf[i, :, b * width:(b + 1) * width] = part[i * each:(i + 1) * each].astype(HALF)

    loads[0].wait()
    rows = qs.shape[1]
    width = l_buf.shape[1]
    for b in range(n_blocks):
        loads[1 + b].wait()
        part = dot(q_buf[...], l_buf[b], NT)
        for i in range(n_layer):
            qs[i, :, b * width:(b + 1) * width] = part[i * rows:(i + 1) * rows].astype(HALF)

    pl.semaphore_wait(barrier, n_layer + n_land - 2)

    copies = over_layer(0, lambda p: qs.at[p], lambda k: qr.at[k - 1])
    loads[2 + n_blocks].wait()
    project(0)
    total = qs[layer].astype(FULL)
    for k, copy in enumerate(copies):
        copy.wait_recv()
        total += qr[k].astype(FULL)
    sent += copies

    hs[...] = total
    copies = over_land(0, lambda p: hs, lambda k: hr.at[k - 1])
    project(1)
    for k, copy in enumerate(copies):
        copy.wait_recv()
        total += hr[k]
    sent += copies

    loads[1 + n_blocks].wait()
    white = dot(total.astype(HALF), w_buf[...], NN).astype(HALF)
    back = dot(white, w_buf[...], NT)
    us[...] = back
    copies = over_land(1, lambda p: us, lambda k: ur.at[k - 1])
    project(2)
    for k, copy in enumerate(copies):
        copy.wait_recv()
        back += ur[k]
    sent += copies

    bs[...] = back.astype(HALF)
    copies = over_layer(1, lambda p: bs, lambda k: br.at[layer])
    br[layer] = bs[...]
    project(3)
    for copy in copies:
        copy.wait_recv()
    sent += copies

    folded = jnp.concatenate([br[i].astype(FULL) for i in range(n_layer)], axis=0).astype(HALF)
    share = out_ref.shape[0]
    copies = []
    for k in list(range(1, n_layer)) + [0]:
        peer = layer_peer(k)
        block = dot(folded, p_buf[peer], NT) * factor
        for j in range(n_land):
            ss[k, j] = block[j * share:(j + 1) * share].astype(HALF)
        for kj in range(n_land):
            if k or kj:
                other = land_peer(kj)
                copy = pltpu.make_async_remote_copy(
                    src_ref=ss.at[k, other], dst_ref=sr.at[k, kj],
                    send_sem=score_send.at[k, kj], recv_sem=score_recv.at[k, kj],
                    device_id=(peer, other), device_id_type=pl.DeviceIdType.MESH)
                copy.start()
                copies.append((k, kj, copy))
    result = ss[0, land].astype(FULL)
    for k, kj, copy in copies[::-1]:
        copy.wait_recv()
        result += sr[k, kj].astype(FULL)
        sent.append(copy)
    out_ref[...] = result

    for copy in sent:
        copy.wait_send()


def fused(gradients, queries, landmarks, whitening):
    n_layer = lax.axis_size("layer")
    n_land = lax.axis_size("land")
    n_rows, width = gradients.shape
    n_query = queries.shape[0]
    n_mark = landmarks.shape[0]
    n_blocks = 4
    each, rows, share = n_rows // n_layer, n_query // n_layer, n_query // n_land
    any_space = pl.BlockSpec(memory_space=pltpu.HBM)
    return pl.pallas_call(
        functools.partial(kernel, n_layer, n_land, n_mark ** (-0.5)),
        out_shape=jax.ShapeDtypeStruct((share, each), FULL),
        in_specs=[any_space] * 4,
        out_specs=pl.BlockSpec(memory_space=pltpu.VMEM),
        scratch_shapes=[
            pltpu.VMEM((n_rows, width), HALF),
            pltpu.VMEM((n_layer, each, n_mark), HALF),
            pltpu.VMEM((n_query, width), HALF),
            pltpu.VMEM((n_blocks, n_mark // n_blocks, width), HALF),
            pltpu.VMEM(whitening.shape, HALF),
            pltpu.SemaphoreType.DMA((n_blocks + 3,)),
            pltpu.VMEM((n_layer, rows, n_mark), HALF),
            pltpu.VMEM((n_layer - 1, rows, n_mark), HALF),
            pltpu.VMEM((rows, n_mark), FULL),
            pltpu.VMEM((n_land - 1, rows, n_mark), FULL),
            pltpu.VMEM((rows, n_mark), FULL),
            pltpu.VMEM((n_land - 1, rows, n_mark), FULL),
            pltpu.VMEM((rows, n_mark), HALF),
            pltpu.VMEM((n_layer, rows, n_mark), HALF),
            pltpu.VMEM((n_layer, n_land, share, each), HALF),
            pltpu.VMEM((n_layer, n_land, share, each), HALF),
            pltpu.SemaphoreType.DMA((2, n_layer - 1)),
            pltpu.SemaphoreType.DMA((2, n_layer - 1)),
            pltpu.SemaphoreType.DMA((2, n_land - 1)),
            pltpu.SemaphoreType.DMA((2, n_land - 1)),
            pltpu.SemaphoreType.DMA((n_layer, n_land)),
            pltpu.SemaphoreType.DMA((n_layer, n_land)),
        ],
        compiler_params=pltpu.CompilerParams(
            collective_id=0, has_side_effects=True, vmem_limit_bytes=63 << 20
        ),
    )(
        gradients,
        queries,
        landmarks.reshape(n_blocks, n_mark // n_blocks, width),
        whitening,
    )


def staged(gradients, queries, landmarks, whitening):
    factor = landmarks.shape[0] ** (-0.5)
    partial = dot(queries, landmarks, NT).astype(HALF)
    query_proj = lax.psum(partial, ("layer", "land"))
    query_white = dot(query_proj, whitening, NN).astype(HALF)
    back = lax.psum(dot(query_white, whitening, NT).astype(HALF), "land")
    spread = dot(back, landmarks, NN).astype(HALF)
    scores = dot(spread, gradients, NT) * factor
    share = lax.psum_scatter(
        scores.astype(HALF), "layer", scatter_dimension=1, tiled=True
    )
    return lax.psum_scatter(share, "land", scatter_dimension=0, tiled=True).astype(FULL)


def local(gradients, queries, landmarks, whitening):
    held = 2 * (gradients.size + queries.size + landmarks.size + whitening.size)
    few = lax.axis_size("layer") * lax.axis_size("land") <= 64
    if few and held <= (24 << 20) and gradients.shape[1] % 128 == 0:
        return fused(gradients, queries, landmarks, whitening)
    return staged(gradients, queries, landmarks, whitening)


def solution(mesh):
    return jax.shard_map(
        local,
        mesh=mesh,
        in_specs=(
            P(None, ("layer", "land")),
            P(None, ("layer", "land")),
            P(None, ("layer", "land")),
            P(None, "land"),
        ),
        out_specs=P("land", "layer"),
        check_vma=False,
    )
```

```python
import functools
import jax
import jax.numpy as jnp
from jax import lax
from jax.experimental import pallas as pl
from jax.experimental.pallas import tpu as pltpu
from jax.sharding import PartitionSpec as P

NN = (((1,), (0,)), ((), ()))
NT = (((1,), (1,)), ((), ()))
HALF = jnp.bfloat16
FULL = jnp.float32


def dot(a, b, dims):
    return lax.dot_general(a, b, dims, preferred_element_type=FULL)


def kernel(
    n_layer, n_land, factor,
    g_hbm, q_hbm, l_hbm, w_hbm, out_ref,
    g_buf, p_buf, q_buf, l_buf, w_buf, load_sem,
    qs, qr, hs, hr, us, ur, bs, br, ss, sr,
    layer_send, layer_recv, land_send, land_recv, score_send, score_recv,
):
    layer = lax.axis_index("layer")
    land = lax.axis_index("land")
    n_blocks = l_buf.shape[0]

    loads = [pltpu.make_async_copy(q_hbm, q_buf, load_sem.at[0])]
    for b in range(n_blocks):
        loads.append(pltpu.make_async_copy(l_hbm.at[b], l_buf.at[b], load_sem.at[1 + b]))
    loads.append(pltpu.make_async_copy(w_hbm, w_buf, load_sem.at[1 + n_blocks]))
    loads.append(pltpu.make_async_copy(g_hbm, g_buf, load_sem.at[2 + n_blocks]))
    for load in loads:
        load.start()

    def layer_peer(k):
        return lax.rem(layer + k, n_layer)

    def land_peer(k):
        return lax.rem(land + k, n_land)

    barrier = pltpu.get_barrier_semaphore()
    for k in range(1, n_layer):
        pl.semaphore_signal(barrier, inc=1, device_id=(layer_peer(k), land),
                            device_id_type=pl.DeviceIdType.MESH)
    for k in range(1, n_land):
        pl.semaphore_signal(barrier, inc=1, device_id=(layer, land_peer(k)),
                            device_id_type=pl.DeviceIdType.MESH)

    far = sorted(range(1, n_layer), key=lambda k: -abs(2 * k - n_layer))

    def over_layer(phase, source, target):
        copies = {}
        for k in far:
            peer = layer_peer(k)
            copy = pltpu.make_async_remote_copy(
                src_ref=source(peer), dst_ref=target(k),
                send_sem=layer_send.at[phase, k - 1],
                recv_sem=layer_recv.at[phase, k - 1],
                device_id=(peer, land), device_id_type=pl.DeviceIdType.MESH)
            copy.start()
            copies[k] = copy
        return [copies[k] for k in range(1, n_layer)]

    def over_land(phase, source, target):
        copies = []
        for k in range(1, n_land):
            peer = land_peer(k)
            copy = pltpu.make_async_remote_copy(
                src_ref=source(peer), dst_ref=target(k),
                send_sem=land_send.at[phase, k - 1],
                recv_sem=land_recv.at[phase, k - 1],
                device_id=(layer, peer), device_id_type=pl.DeviceIdType.MESH)
            copy.start()
            copies.append(copy)
        return copies

    sent = []
    each = p_buf.shape[1]

    def project(b):
        part = dot(g_buf[...], l_buf[b], NT)
        for i in range(n_layer):
            p_buf[i, :, b * width:(b + 1) * width] = part[i * each:(i + 1) * each].astype(HALF)

    loads[0].wait()
    rows = qs.shape[1]
    width = l_buf.shape[1]
    for b in range(n_blocks):
        loads[1 + b].wait()
        part = dot(q_buf[...], l_buf[b], NT)
        for i in range(n_layer):
            qs[i, :, b * width:(b + 1) * width] = part[i * rows:(i + 1) * rows].astype(HALF)

    pl.semaphore_wait(barrier, n_layer + n_land - 2)

    copies = over_layer(0, lambda p: qs.at[p], lambda k: qr.at[k - 1])
    loads[2 + n_blocks].wait()
    project(0)
    total = qs[layer].astype(FULL)
    for k, copy in enumerate(copies):
        copy.wait_recv()
        total += qr[k].astype(FULL)
    sent += copies

    hs[...] = total.astype(HALF)
    copies = over_land(0, lambda p: hs, lambda k: hr.at[k - 1])
    project(1)
    for k, copy in enumerate(copies):
        copy.wait_recv()
        total += hr[k].astype(FULL)
    sent += copies

    loads[1 + n_blocks].wait()
    white = dot(total.astype(HALF), w_buf[...], NN).astype(HALF)
    back = dot(white, w_buf[...], NT)
    us[...] = back.astype(HALF)
    copies = over_land(1, lambda p: us, lambda k: ur.at[k - 1])
    project(2)
    for k, copy in enumerate(copies):
        copy.wait_recv()
        back += ur[k].astype(FULL)
    sent += copies

    bs[...] = back.astype(HALF)
    copies = over_layer(1, lambda p: bs, lambda k: br.at[layer])
    br[layer] = bs[...]
    project(3)
    for copy in copies:
        copy.wait_recv()
    sent += copies

    folded = jnp.concatenate([br[i].astype(FULL) for i in range(n_layer)], axis=0).astype(HALF)
    share = out_ref.shape[0]
    copies = []
    for k in far + [0]:
        peer = layer_peer(k)
        block = dot(folded, p_buf[peer], NT) * factor
        for j in range(n_land):
            ss[k, j] = block[j * share:(j + 1) * share].astype(HALF)
        for kj in range(n_land):
            if k or kj:
                other = land_peer(kj)
                copy = pltpu.make_async_remote_copy(
                    src_ref=ss.at[k, other], dst_ref=sr.at[k, kj],
                    send_sem=score_send.at[k, kj], recv_sem=score_recv.at[k, kj],
                    device_id=(peer, other), device_id_type=pl.DeviceIdType.MESH)
                copy.start()
                copies.append((k, kj, copy))
    result = ss[0, land].astype(FULL)
    for k, kj, copy in copies[::-1]:
        copy.wait_recv()
        result += sr[k, kj].astype(FULL)
        sent.append(copy)
    out_ref[...] = result

    for copy in sent:
        copy.wait_send()


def fused(gradients, queries, landmarks, whitening):
    n_layer = lax.axis_size("layer")
    n_land = lax.axis_size("land")
    n_rows, width = gradients.shape
    n_query = queries.shape[0]
    n_mark = landmarks.shape[0]
    n_blocks = 4
    each, rows, share = n_rows // n_layer, n_query // n_layer, n_query // n_land
    any_space = pl.BlockSpec(memory_space=pltpu.HBM)
    return pl.pallas_call(
        functools.partial(kernel, n_layer, n_land, n_mark ** (-0.5)),
        out_shape=jax.ShapeDtypeStruct((share, each), FULL),
        in_specs=[any_space] * 4,
        out_specs=pl.BlockSpec(memory_space=pltpu.VMEM),
        scratch_shapes=[
            pltpu.VMEM((n_rows, width), HALF),
            pltpu.VMEM((n_layer, each, n_mark), HALF),
            pltpu.VMEM((n_query, width), HALF),
            pltpu.VMEM((n_blocks, n_mark // n_blocks, width), HALF),
            pltpu.VMEM(whitening.shape, HALF),
            pltpu.SemaphoreType.DMA((n_blocks + 3,)),
            pltpu.VMEM((n_layer, rows, n_mark), HALF),
            pltpu.VMEM((n_layer - 1, rows, n_mark), HALF),
            pltpu.VMEM((rows, n_mark), HALF),
            pltpu.VMEM((n_land - 1, rows, n_mark), HALF),
            pltpu.VMEM((rows, n_mark), HALF),
            pltpu.VMEM((n_land - 1, rows, n_mark), HALF),
            pltpu.VMEM((rows, n_mark), HALF),
            pltpu.VMEM((n_layer, rows, n_mark), HALF),
            pltpu.VMEM((n_layer, n_land, share, each), HALF),
            pltpu.VMEM((n_layer, n_land, share, each), HALF),
            pltpu.SemaphoreType.DMA((2, n_layer - 1)),
            pltpu.SemaphoreType.DMA((2, n_layer - 1)),
            pltpu.SemaphoreType.DMA((2, n_land - 1)),
            pltpu.SemaphoreType.DMA((2, n_land - 1)),
            pltpu.SemaphoreType.DMA((n_layer, n_land)),
            pltpu.SemaphoreType.DMA((n_layer, n_land)),
        ],
        compiler_params=pltpu.CompilerParams(
            collective_id=0, has_side_effects=True, vmem_limit_bytes=63 << 20
        ),
    )(
        gradients,
        queries,
        landmarks.reshape(n_blocks, n_mark // n_blocks, width),
        whitening,
    )


def staged(gradients, queries, landmarks, whitening):
    factor = landmarks.shape[0] ** (-0.5)
    partial = dot(queries, landmarks, NT).astype(HALF)
    query_proj = lax.psum(partial, ("layer", "land"))
    query_white = dot(query_proj, whitening, NN).astype(HALF)
    back = lax.psum(dot(query_white, whitening, NT).astype(HALF), "land")
    spread = dot(back, landmarks, NN).astype(HALF)
    scores = dot(spread, gradients, NT) * factor
    share = lax.psum_scatter(
        scores.astype(HALF), "layer", scatter_dimension=1, tiled=True
    )
    return lax.psum_scatter(share, "land", scatter_dimension=0, tiled=True).astype(FULL)


def local(gradients, queries, landmarks, whitening):
    held = 2 * (gradients.size + queries.size + landmarks.size + whitening.size)
    few = lax.axis_size("layer") * lax.axis_size("land") <= 64
    if few and held <= (24 << 20) and gradients.shape[1] % 128 == 0:
        return fused(gradients, queries, landmarks, whitening)
    return staged(gradients, queries, landmarks, whitening)


def solution(mesh):
    return jax.shard_map(
        local,
        mesh=mesh,
        in_specs=(
            P(None, ("layer", "land")),
            P(None, ("layer", "land")),
            P(None, ("layer", "land")),
            P(None, "land"),
        ),
        out_specs=P("land", "layer"),
        check_vma=False,
    )
```
